32 devices in a mesh: layer: 4 (over x, core), row: 2 (over y), col: 4 (over z).
Axes of the slice: x: 2, y: 2, z: 4, core: 2. Of those that a mesh axis runs over, the one named last changes fastest.
Arguments:
- schur_window: float32 [4, 2, 256, 2, 4, 256], P(None, 'row', None, None, 'col'), may hold values from -8 to 24, as said below
Outputs:
- factored: float32 [4, 2, 256, 2, 4, 256], P(None, 'row', 'layer', None, 'col')
The draws below stay inside these ranges and needn't reach their ends.
Inputs may be any that keep to these rules, and one draw needn't show every extreme that they name: `schur_window`: the leading 2048 columns of a symmetric positive definite matrix: its leading 2048 x 2048 block is symmetric and positive definite.
All inputs are finite; a program needn't handle non-finite values.
Results may differ from the reference program's by a relative error of at most 0.0001.
Values sent between devices are 32-bit elements; how exact they have to be, the bound alone decides.
A program may use at most 64 MiB of HBM per device.

```python
import math
import jax
import jax.numpy as jnp
from jax import lax

PANEL = 256
PANELS = 2
ROW_BLOCKS = 4
COL_BLOCKS = 2
ROWS = 2048
COLS = 2048
N_ROW = 2
N_COL = 4


def draw_schur_window(key, part):
    row_total = ROW_BLOCKS * N_ROW * PANEL
    col_total = COL_BLOCKS * N_COL * PANEL
    rank_total = PANELS * PANEL
    noise_key, factor_key, diagonal_key = jax.random.split(key, 3)
    rough_part = jax.random.normal(noise_key, (row_total, col_total), jnp.float32)
    factor_draw = jax.random.normal(factor_key, (row_total, rank_total), jnp.float32)
    upper_noise = rough_part[:col_total]
    symmetric_top = (upper_noise + upper_noise.T) * 0.7071067811865476
    rough_part = jnp.concatenate([symmetric_top, rough_part[col_total:]], axis=0) * (0.25 / math.sqrt(col_total))
    coupling = jnp.dot(factor_draw, factor_draw[:col_total].T, precision=lax.Precision.HIGHEST) * (4.0 / rank_total)
    diagonal = jax.random.uniform(diagonal_key, (col_total,), jnp.float32, 2.0, 4.0)
    positions = jnp.arange(col_total, dtype=jnp.int32)
    matrix_draw = (rough_part + coupling).at[positions, positions].add(diagonal)
    return matrix_draw.reshape(ROW_BLOCKS, N_ROW, PANEL, COL_BLOCKS, N_COL, PANEL)


def setup_inputs(seed: int = 0) -> dict:
    streams_of = jax.random.split(jax.random.key(seed), 2)
    return {
        "schur_window": draw_schur_window(jax.random.fold_in(streams_of[1], 71), 0),
    }


def reference(schur_window):
    matrix = schur_window.reshape(ROWS, COLS)
    row_block = (jnp.arange(ROWS, dtype=jnp.int32) // PANEL)[:, None]
    for panel_index in range(PANELS):
        block_start = panel_index * PANEL
        block_end = block_start + PANEL
        factor = jnp.linalg.cholesky(matrix[block_start:block_end, block_start:block_end])
        solved = jax.scipy.linalg.solve_triangular(factor, matrix[:, block_start:block_end].T, lower=True).T
        column = jnp.where(row_block > panel_index, solved, jnp.zeros_like(solved))
        column = column.at[block_start:block_end].set(factor)
        update = jnp.dot(column[block_end:].astype(jnp.float32), column[block_end:COLS].T.astype(jnp.float32), precision=lax.Precision.HIGHEST, preferred_element_type=jnp.float32)
        matrix = matrix.at[block_end:, block_end:].add(-update)
        matrix = matrix.at[:, block_start:block_end].set(column)
        matrix = matrix.at[block_start:block_end, block_end:].set(jnp.zeros((PANEL, COLS - block_end), jnp.float32))
    return matrix.reshape(schur_window.shape)
```

```python
import functools

import jax
import jax.numpy as jnp
from jax import lax
from jax.experimental import pallas as pl
from jax.experimental.pallas import tpu as pltpu
from jax.sharding import PartitionSpec as P

PANELS = 2
GROUP = 8
BLOCKS = ((0, 0), (1, 0), (1, 1))


def dot(a, b, lhs, rhs):
    return lax.dot_general(
        a, b, (((lhs,), (rhs,)), ((), ())),
        precision=lax.Precision.HIGHEST, preferred_element_type=jnp.float32,
    )


def matmul(a, b):
    return dot(a, b, 1, 0)


def matmul_t(a, b):
    return dot(a, b, 1, 1)


def eliminate(aug, half):
    lane = lax.broadcasted_iota(jnp.int32, (GROUP, half), 1)
    sub = lax.broadcasted_iota(jnp.int32, (GROUP, 2 * half), 0)

    def step(s, carry):
        first = pl.multiple_of(s * GROUP, GROUP)
        block = aug[pl.ds(first, GROUP), :]
        turned = pltpu.roll(block[:, :half], lax.rem(half - first, half), 1)
        rows = [jnp.broadcast_to(block[j : j + 1, :], (GROUP, 2 * half)) for j in range(GROUP)]
        entry = [
            [jnp.broadcast_to(turned[j : j + 1, k : k + 1], (GROUP, half)) if k >= j else None for k in range(GROUP)]
            for j in range(GROUP)
        ]
        done = jnp.zeros((GROUP, 2 * half), jnp.float32)
        for j in range(GROUP):
            scale = lax.rsqrt(entry[j][j])
            row = rows[j] * jnp.concatenate([scale, scale], axis=1)
            done = jnp.where(sub == j, row, done)
            low = [entry[j][k] * scale if k > j else None for k in range(GROUP)]
            for k in range(j + 1, GROUP):
                for m in range(k, GROUP):
                    entry[k][m] = entry[k][m] - low[k] * low[m]
                rows[k] = rows[k] - jnp.concatenate([low[k], low[k]], axis=1) * row
        later = jnp.where(lane >= first + GROUP, done[:, :half], 0.0)
        aug[...] -= dot(later, done, 0, 0)
        aug[pl.ds(first, GROUP), :] = done
        return carry

    lax.fori_loop(0, half // GROUP, step, 0)


def factor_panel(block, aug, factor, inverse, width):
    half = width // 2
    row = lax.broadcasted_iota(jnp.int32, (half, half), 0)
    col = lax.broadcasted_iota(jnp.int32, (half, half), 1)
    eye = jnp.where(row == col, 1.0, 0.0).astype(jnp.float32)
    zero = jnp.zeros((half, half), jnp.float32)

    def diagonal(value):
        aug[:, :half] = value
        aug[:, half:] = eye
        eliminate(aug, half)
        return jnp.where(row <= col, aug[:, :half], 0.0).T, aug[:, half:]

    low1, inv1 = diagonal(block[:half, :half])
    factor[:half, :half] = low1
    inverse[:half, :half] = inv1
    factor[:half, half:] = zero
    inverse[:half, half:] = zero
    below = matmul_t(block[half:, :half], inv1)
    factor[half:, :half] = below
    low2, inv2 = diagonal(block[half:, half:] - matmul_t(below, below))
    factor[half:, half:] = low2
    inverse[half:, half:] = inv2
    inverse[half:, :half] = -matmul(inv2, matmul(below, inverse[:half, :half]))


def kernel(
    sizes, top, share, out, diag, across, panel, aug, factor, inverse, cross, rest, left,
    diag_send, diag_recv, pass_send, pass_recv, across_send, across_recv, panel_send, panel_recv, local_sem,
):
    layers, grid_rows, grid_cols, row_blocks, col_blocks, width = sizes
    rows_here = width // layers
    me_layer, me_row, me_col = lax.axis_index("layer"), lax.axis_index("row"), lax.axis_index("col")

    def at(layer, row, col):
        return (lax.rem(me_layer + layer, layers), lax.rem(me_row + row, grid_rows), lax.rem(me_col + col, grid_cols))

    def remote(src, dst, send, recv, target):
        return pltpu.make_async_remote_copy(
            src_ref=src, dst_ref=dst, send_sem=send, recv_sem=recv, device_id=target,
            device_id_type=pl.DeviceIdType.MESH,
        )

    grid_peers = [(row, col) for row in range(grid_rows) for col in range(grid_cols) if row or col]
    barrier = pltpu.get_barrier_semaphore()
    for row, col in grid_peers:
        pl.semaphore_signal(barrier, inc=1, device_id=at(0, row, col), device_id_type=pl.DeviceIdType.MESH)
    for layer in range(1, layers):
        pl.semaphore_signal(barrier, inc=1, device_id=at(layer, 0, 0), device_id_type=pl.DeviceIdType.MESH)
    pl.semaphore_wait(barrier, len(grid_peers) + layers - 1)

    def stripe(layer):
        return pl.ds(pl.multiple_of(layer * rows_here, rows_here), rows_here)

    def diag_copy(b, n):
        src = top.at[stripe(me_layer), pl.ds(0, width)]
        dst = diag.at[b, stripe(me_layer), :]
        return remote(src, dst, diag_send.at[b, n], diag_recv.at[b], at(0, *grid_peers[n]))

    def diag_local(b):
        return pltpu.make_async_copy(
            top.at[stripe(me_layer), pl.ds(0, width)], diag.at[b, stripe(me_layer), :], local_sem.at[b]
        )

    def pass_copy(b, n):
        part = diag.at[b, stripe(me_layer), :]
        return remote(part, part, pass_send.at[b, n - 1], pass_recv.at[b, n - 1], at(n, 0, 0))

    def across_copy(k, n):
        return remote(top, across.at[k], across_send.at[k, n - 1], across_recv.at[k], at(0, n, 0))

    def across_local(k):
        return pltpu.make_async_copy(top, across.at[k], local_sem.at[len(BLOCKS) + k])

    def panel_copy(k, n):
        return remote(share.at[:, pl.ds(0, width)], panel.at[k], panel_send.at[k, n - 1], panel_recv.at[k], at(0, 0, n))

    def panel_local(k):
        return pltpu.make_async_copy(
            share.at[:, pl.ds(0, width)], panel.at[k], local_sem.at[len(BLOCKS) + PANELS + k]
        )

    owners = [(me_row == i) & (me_col == j) for i, j in BLOCKS]
    for b in range(len(BLOCKS)):

        @pl.when(owners[b])
        def _(b=b):
            for n in range(len(grid_peers)):
                diag_copy(b, n).start()
            diag_local(b).start()

    for k in range(PANELS):

        @pl.when(me_col == k)
        def _(k=k):
            for n in range(1, grid_cols):
                panel_copy(k, n).start()
            panel_local(k).start()

        @pl.when(me_row == k)
        def _(k=k):
            for n in range(1, grid_rows):
                across_copy(k, n).start()
            across_local(k).start()

    for b in range(len(BLOCKS)):

        @pl.when(owners[b])
        def _(b=b):
            diag_local(b).wait()

        @pl.when(jnp.logical_not(owners[b]))
        def _(b=b):
            diag_copy(b, 0).wait_recv()

        for n in range(1, layers):
            pass_copy(b, n).start()

    def diag_arrived(b):
        for n in range(1, layers):
            pass_copy(b, n).wait_recv()

    diag_arrived(0)
    factor_panel(diag.at[0], aug, factor.at[0], inverse.at[0], width)
    diag_arrived(1)
    cross[...] = matmul_t(diag[1], inverse[0])
    diag_arrived(2)
    rest[...] = diag[2] - matmul_t(cross[...], cross[...])
    factor_panel(rest, aug, factor.at[1], inverse.at[1], width)

    for k in range(PANELS):

        @pl.when(me_col == k)
        def _(k=k):
            panel_local(k).wait()

        @pl.when(me_col != k)
        def _(k=k):
            panel_copy(k, 1).wait_recv()

        @pl.when(me_row == k)
        def _(k=k):
            across_local(k).wait()

        @pl.when(me_row != k)
        def _(k=k):
            across_copy(k, 1).wait_recv()

    left[0] = matmul_t(panel[0], inverse[0])
    left[1] = matmul_t(panel[1] - matmul_t(left[0], cross[...]), inverse[1])
    right0 = matmul(inverse[0], across[0])
    right1 = matmul(inverse[1], across[1] - matmul(cross[...], right0))
    here = stripe(me_layer)
    first0 = jnp.where(me_row == 0, factor[0, here, :], left[0, :rows_here, :])
    first1 = jnp.where(me_row == 0, 0.0, jnp.where(me_row == 1, factor[1, here, :], left[1, :rows_here, :]))
    updated = share[...] - matmul(left[0], right0) - matmul(left[1], right1)
    for slot in range(col_blocks):
        number = slot * grid_cols + me_col
        columns = slice(slot * width, (slot + 1) * width)
        out[:, columns] = jnp.where(number == 0, left[0], jnp.where(number == 1, left[1], updated[:, columns]))
        plain = jnp.where(me_row < PANELS, 0.0, updated[:rows_here, columns])
        out[:rows_here, columns] = jnp.where(number == 0, first0, jnp.where(number == 1, first1, plain))

    for b in range(len(BLOCKS)):

        @pl.when(owners[b])
        def _(b=b):
            for n in range(len(grid_peers)):
                diag_copy(b, n).wait_send()

        for n in range(1, layers):
            pass_copy(b, n).wait_send()
    for k in range(PANELS):

        @pl.when(me_col == k)
        def _(k=k):
            for n in range(1, grid_cols):
                panel_copy(k, n).wait_send()

        @pl.when(me_row == k)
        def _(k=k):
            for n in range(1, grid_rows):
                across_copy(k, n).wait_send()


def local(sizes, schur_window):
    layers, grid_rows, grid_cols, row_blocks, col_blocks, width = sizes
    rows_here = width // layers
    held = schur_window.reshape(row_blocks, width, col_blocks * width)
    share = lax.dynamic_slice_in_dim(held, lax.axis_index("layer") * rows_here, rows_here, 1)
    share = share.reshape(row_blocks * rows_here, col_blocks * width)
    top = held[0]
    vmem = pl.BlockSpec(memory_space=pltpu.VMEM)
    dma = pltpu.SemaphoreType.DMA
    diagonals, peers, half = len(BLOCKS), grid_rows * grid_cols - 1, width // 2
    f32 = jnp.float32
    result = pl.pallas_call(
        functools.partial(kernel, sizes),
        out_shape=jax.ShapeDtypeStruct(share.shape, f32),
        in_specs=[vmem, vmem],
        out_specs=vmem,
        scratch_shapes=[
            pltpu.VMEM((diagonals, width, width), f32),
            pltpu.VMEM((PANELS, width, col_blocks * width), f32),
            pltpu.VMEM((PANELS, row_blocks * rows_here, width), f32),
            pltpu.VMEM((half, width), f32),
            pltpu.VMEM((PANELS, width, width), f32),
            pltpu.VMEM((PANELS, width, width), f32),
            pltpu.VMEM((width, width), f32),
            pltpu.VMEM((width, width), f32),
            pltpu.VMEM((PANELS, row_blocks * rows_here, width), f32),
            dma((diagonals, peers)),
            dma((diagonals,)),
            dma((diagonals, layers - 1)),
            dma((diagonals, layers - 1)),
            dma((PANELS, grid_rows - 1)),
            dma((PANELS,)),
            dma((PANELS, grid_cols - 1)),
            dma((PANELS,)),
            dma((diagonals + 2 * PANELS,)),
        ],
        compiler_params=pltpu.CompilerParams(collective_id=0, has_side_effects=True),
        name="window",
    )(top, share)
    return result.reshape(row_blocks, 1, rows_here, col_blocks, 1, width)


def solution(mesh):
    def body(schur_window):
        row_blocks, _, width, col_blocks, _, _ = schur_window.shape
        sizes = (mesh.shape["layer"], mesh.shape["row"], mesh.shape["col"], row_blocks, col_blocks, width)
        return local(sizes, schur_window)

    return jax.shard_map(
        body,
        mesh=mesh,
        in_specs=(P(None, "row", None, None, "col", None),),
        out_specs=P(None, "row", "layer", None, "col", None),
        check_vma=False,
    )
```

```python
import functools

import jax
import jax.numpy as jnp
from jax import lax
from jax.experimental import pallas as pl
from jax.experimental.pallas import tpu as pltpu
from jax.sharding import PartitionSpec as P

PANELS = 2
GROUP = 8
BLOCKS = ((0, 0), (1, 0), (1, 1))


def dot(a, b, lhs, rhs):
    return lax.dot_general(
        a, b, (((lhs,), (rhs,)), ((), ())),
        precision=lax.Precision.HIGHEST, preferred_element_type=jnp.float32,
    )


def matmul(a, b):
    return dot(a, b, 1, 0)


def matmul_t(a, b):
    return dot(a, b, 1, 1)


def eliminate(aug, half):
    lane = lax.broadcasted_iota(jnp.int32, (GROUP, half), 1)
    sub = lax.broadcasted_iota(jnp.int32, (GROUP, 2 * half), 0)

    def step(s, carry):
        first = pl.multiple_of(s * GROUP, GROUP)
        block = aug[pl.ds(first, GROUP), :]
        turned = pltpu.roll(block[:, :half], lax.rem(half - first, half), 1)
        rows = [jnp.broadcast_to(block[j : j + 1, :], (GROUP, 2 * half)) for j in range(GROUP)]
        entry = [
            [jnp.broadcast_to(turned[j : j + 1, k : k + 1], (GROUP, half)) if k >= j else None for k in range(GROUP)]
            for j in range(GROUP)
        ]
        done = jnp.zeros((GROUP, 2 * half), jnp.float32)
        for j in range(GROUP):
            scale = lax.rsqrt(entry[j][j])
            row = rows[j] * jnp.concatenate([scale, scale], axis=1)
            done = jnp.where(sub == j, row, done)
            low = [entry[j][k] * scale if k > j else None for k in range(GROUP)]
            for k in range(j + 1, GROUP):
                for m in range(k, GROUP):
                    entry[k][m] = entry[k][m] - low[k] * low[m]
                rows[k] = rows[k] - jnp.concatenate([low[k], low[k]], axis=1) * row
        later = jnp.where(lane >= first + GROUP, done[:, :half], 0.0)
        aug[...] -= dot(later, done, 0, 0)
        aug[pl.ds(first, GROUP), :] = done
        return carry

    lax.fori_loop(0, half // GROUP, step, 0)


def factor_panel(block, aug, factor, inverse, width):
    half = width // 2
    row = lax.broadcasted_iota(jnp.int32, (half, half), 0)
    col = lax.broadcasted_iota(jnp.int32, (half, half), 1)
    eye = jnp.where(row == col, 1.0, 0.0).astype(jnp.float32)
    zero = jnp.zeros((half, half), jnp.float32)

    def diagonal(value):
        aug[:, :half] = value
        aug[:, half:] = eye
        eliminate(aug, half)
        return jnp.where(row <= col, aug[:, :half], 0.0).T, aug[:, half:]

    low1, inv1 = diagonal(block[:half, :half])
    factor[:half, :half] = low1
    inverse[:half, :half] = inv1
    factor[:half, half:] = zero
    inverse[:half, half:] = zero
    below = matmul_t(block[half:, :half], inv1)
    factor[half:, :half] = below
    low2, inv2 = diagonal(block[half:, half:] - matmul_t(below, below))
    factor[half:, half:] = low2
    inverse[half:, half:] = inv2
    inverse[half:, :half] = -matmul(inv2, matmul(below, inverse[:half, :half]))


def kernel(
    sizes, window, out, diag, across, panel, share, staged, aug, factor, inverse, cross, rest, left,
    diag_send, diag_recv, pass_send, pass_recv, across_send, across_recv, panel_send, panel_recv, local_sem, share_sem, out_sem,
):
    layers, grid_rows, grid_cols, row_blocks, col_blocks, width = sizes
    rows_here = width // layers
    me_layer, me_row, me_col = lax.axis_index("layer"), lax.axis_index("row"), lax.axis_index("col")

    def at(layer, row, col):
        return (lax.rem(me_layer + layer, layers), lax.rem(me_row + row, grid_rows), lax.rem(me_col + col, grid_cols))

    def remote(src, dst, send, recv, target):
        return pltpu.make_async_remote_copy(
            src_ref=src, dst_ref=dst, send_sem=send, recv_sem=recv, device_id=target,
            device_id_type=pl.DeviceIdType.MESH,
        )

    def stripe(layer):
        return pl.ds(pl.multiple_of(layer * rows_here, rows_here), rows_here)

    here = stripe(me_layer)

    def share_copy(slot):
        return pltpu.make_async_copy(window.at[:, 0, here, slot, 0, :], share.at[slot], share_sem.at[slot])

    grid_peers = [(row, col) for row in range(grid_rows) for col in range(grid_cols) if row or col]
    barrier = pltpu.get_barrier_semaphore()
    for row, col in grid_peers:
        pl.semaphore_signal(barrier, inc=1, device_id=at(0, row, col), device_id_type=pl.DeviceIdType.MESH)
    for layer in range(1, layers):
        pl.semaphore_signal(barrier, inc=1, device_id=at(layer, 0, 0), device_id_type=pl.DeviceIdType.MESH)
    for slot in range(col_blocks):
        share_copy(slot).start()
    pl.semaphore_wait(barrier, len(grid_peers) + layers - 1)

    diag_src = window.at[0, 0, here, 0, 0, :]

    def diag_copy(b, n):
        return remote(diag_src, diag.at[b, here, :], diag_send.at[b, n], diag_recv.at[b], at(0, *grid_peers[n]))

    def diag_local(b):
        return pltpu.make_async_copy(diag_src, diag.at[b, here, :], local_sem.at[b])

    def pass_copy(b, n):
        part = diag.at[b, here, :]
        return remote(part, part, pass_send.at[b, n - 1], pass_recv.at[b, n - 1], at(n, 0, 0))

    def across_copy(k, slot, n):
        return remote(
            window.at[0, 0, :, slot, 0, :], across.at[k, slot], across_send.at[k, slot, n - 1],
            across_recv.at[k, slot], at(0, n, 0),
        )

    def across_local(k, slot):
        return pltpu.make_async_copy(window.at[0, 0, :, slot, 0, :], across.at[k, slot], across_recv.at[k, slot])

    panel_src = window.at[:, 0, here, 0, 0, :]

    def panel_copy(k, n):
        return remote(panel_src, panel.at[k], panel_send.at[k, n - 1], panel_recv.at[k], at(0, 0, n))

    def panel_local(k):
        return pltpu.make_async_copy(panel_src, panel.at[k], panel_recv.at[k])

    owners = [(me_row == i) & (me_col == j) for i, j in BLOCKS]
    for b in range(len(BLOCKS)):

        @pl.when(owners[b])
        def _(b=b):
            for n in range(len(grid_peers)):
                diag_copy(b, n).start()
            diag_local(b).start()

    for k in range(PANELS):

        @pl.when(me_col == k)
        def _(k=k):
            for n in range(1, grid_cols):
                panel_copy(k, n).start()
            panel_local(k).start()

        @pl.when(me_row == k)
        def _(k=k):
            for slot in range(col_blocks):
                for n in range(1, grid_rows):
                    across_copy(k, slot, n).start()
                across_local(k, slot).start()

    for b in range(len(BLOCKS)):

        @pl.when(owners[b])
        def _(b=b):
            diag_local(b).wait()

        @pl.when(jnp.logical_not(owners[b]))
        def _(b=b):
            diag_copy(b, 0).wait_recv()

        for n in range(1, layers):
            pass_copy(b, n).start()

    def diag_arrived(b):
        for n in range(1, layers):
            pass_copy(b, n).wait_recv()

    diag_arrived(0)
    factor_panel(diag.at[0], aug, factor.at[0], inverse.at[0], width)
    diag_arrived(1)
    cross[...] = matmul_t(diag[1], inverse[0])
    diag_arrived(2)
    rest[...] = diag[2] - matmul_t(cross[...], cross[...])
    factor_panel(rest, aug, factor.at[1], inverse.at[1], width)

    def panel_arrived(k):
        @pl.when(me_col == k)
        def _():
            panel_local(k).wait()

        @pl.when(me_col != k)
        def _():
            panel_copy(k, 1).wait_recv()

    def across_arrived(k, slot):
        @pl.when(me_row == k)
        def _():
            across_local(k, slot).wait()

        @pl.when(me_row != k)
        def _():
            across_copy(k, slot, 1).wait_recv()

    total = row_blocks * rows_here
    for k in range(PANELS):
        panel_arrived(k)
    left[0] = matmul_t(panel[0].reshape(total, width), inverse[0])
    left[1] = matmul_t(panel[1].reshape(total, width) - matmul_t(left[0], cross[...]), inverse[1])
    first0 = jnp.where(me_row == 0, factor[0, here, :], left[0, :rows_here, :])
    first1 = jnp.where(me_row == 0, 0.0, jnp.where(me_row == 1, factor[1, here, :], left[1, :rows_here, :]))

    def out_copy(slot):
        return pltpu.make_async_copy(staged.at[slot], out.at[:, 0, :, slot, 0, :], out_sem.at[slot])

    for slot in range(col_blocks):
        for k in range(PANELS):
            across_arrived(k, slot)
        share_copy(slot).wait()
        right0 = matmul(inverse[0], across[0, slot])
        right1 = matmul(inverse[1], across[1, slot] - matmul(cross[...], right0))
        updated = share[slot].reshape(total, width) - matmul(left[0], right0) - matmul(left[1], right1)
        number = slot * grid_cols + me_col
        value = jnp.where(number == 0, left[0], jnp.where(number == 1, left[1], updated))
        staged[slot] = value.reshape(row_blocks, rows_here, width)
        plain = jnp.where(me_row < PANELS, 0.0, updated[:rows_here])
        staged[slot, 0] = jnp.where(number == 0, first0, jnp.where(number == 1, first1, plain))
        out_copy(slot).start()

    for b in range(len(BLOCKS)):

        @pl.when(owners[b])
        def _(b=b):
            for n in range(len(grid_peers)):
                diag_copy(b, n).wait_send()

        for n in range(1, layers):
            pass_copy(b, n).wait_send()
    for k in range(PANELS):

        @pl.when(me_col == k)
        def _(k=k):
            for n in range(1, grid_cols):
                panel_copy(k, n).wait_send()

        @pl.when(me_row == k)
        def _(k=k):
            for slot in range(col_blocks):
                for n in range(1, grid_rows):
                    across_copy(k, slot, n).wait_send()
    for slot in range(col_blocks):
        out_copy(slot).wait()


def local(sizes, schur_window):
    layers, grid_rows, grid_cols, row_blocks, col_blocks, width = sizes
    rows_here = width // layers
    anywhere = pl.BlockSpec(memory_space=pl.ANY)
    dma = pltpu.SemaphoreType.DMA
    diagonals, peers, half = len(BLOCKS), grid_rows * grid_cols - 1, width // 2
    f32 = jnp.float32
    return pl.pallas_call(
        functools.partial(kernel, sizes),
        out_shape=jax.ShapeDtypeStruct((row_blocks, 1, rows_here, col_blocks, 1, width), f32),
        in_specs=[anywhere],
        out_specs=anywhere,
        scratch_shapes=[
            pltpu.VMEM((diagonals, width, width), f32),
            pltpu.VMEM((PANELS, col_blocks, width, width), f32),
            pltpu.VMEM((PANELS, row_blocks, rows_here, width), f32),
            pltpu.VMEM((col_blocks, row_blocks, rows_here, width), f32),
            pltpu.VMEM((col_blocks, row_blocks, rows_here, width), f32),
            pltpu.VMEM((half, width), f32),
            pltpu.VMEM((PANELS, width, width), f32),
            pltpu.VMEM((PANELS, width, width), f32),
            pltpu.VMEM((width, width), f32),
            pltpu.VMEM((width, width), f32),
            pltpu.VMEM((PANELS, row_blocks * rows_here, width), f32),
            dma((diagonals, peers)),
            dma((diagonals,)),
            dma((diagonals, layers - 1)),
            dma((diagonals, layers - 1)),
            dma((PANELS, col_blocks, grid_rows - 1)),
            dma((PANELS, col_blocks)),
            dma((PANELS, grid_cols - 1)),
            dma((PANELS,)),
            dma((diagonals,)),
            dma((col_blocks,)),
            dma((col_blocks,)),
        ],
        compiler_params=pltpu.CompilerParams(collective_id=0, has_side_effects=True),
        name="window",
    )(schur_window)


def solution(mesh):
    def body(schur_window):
        row_blocks, _, width, col_blocks, _, _ = schur_window.shape
        sizes = (mesh.shape["layer"], mesh.shape["row"], mesh.shape["col"], row_blocks, col_blocks, width)
        return local(sizes, schur_window)

    return jax.shard_map(
        body,
        mesh=mesh,
        in_specs=(P(None, "row", None, None, "col", None),),
        out_specs=P(None, "row", "layer", None, "col", None),
        check_vma=False,
    )
```

```python
import functools

import jax
import jax.numpy as jnp
from jax import lax
from jax.experimental import pallas as pl
from jax.experimental.pallas import tpu as pltpu
from jax.sharding import PartitionSpec as P

PANELS = 2
GROUP = 8
BLOCKS = ((0, 0), (1, 0), (1, 1))


def dot(a, b, lhs, rhs):
    return lax.dot_general(
        a, b, (((lhs,), (rhs,)), ((), ())),
        precision=lax.Precision.HIGHEST, preferred_element_type=jnp.float32,
    )


def matmul(a, b):
    return dot(a, b, 1, 0)


def matmul_t(a, b):
    return dot(a, b, 1, 1)


def parts(value):
    high = value.astype(jnp.bfloat16).astype(jnp.float32)
    mid = (value - high).astype(jnp.bfloat16).astype(jnp.float32)
    return high, mid, value - high - mid


def eliminate(aug, half):
    lane = lax.broadcasted_iota(jnp.int32, (GROUP, half), 1)
    sub = lax.broadcasted_iota(jnp.int32, (GROUP, 2 * half), 0)

    def step(start, s, carry):
        first = pl.multiple_of(s * GROUP, GROUP)
        block = aug[pl.ds(first, GROUP), :]
        turned = pltpu.roll(block[:, :half], lax.rem(half - first, half), 1)
        rows = [jnp.broadcast_to(block[j : j + 1, :], (GROUP, 2 * half)) for j in range(GROUP)]
        entry = [
            [jnp.broadcast_to(turned[j : j + 1, k : k + 1], (GROUP, half)) if k >= j else None for k in range(GROUP)]
            for j in range(GROUP)
        ]
        done = jnp.zeros((GROUP, 2 * half), jnp.float32)
        for j in range(GROUP):
            scale = lax.rsqrt(entry[j][j])
            row = rows[j] * jnp.concatenate([scale, scale], axis=1)
            done = jnp.where(sub == j, row, done)
            low = [entry[j][k] * scale if k > j else None for k in range(GROUP)]
            for k in range(j + 1, GROUP):
                for m in range(k, GROUP):
                    entry[k][m] = entry[k][m] - low[k] * low[m]
                rows[k] = rows[k] - jnp.concatenate([low[k], low[k]], axis=1) * row
        later = jnp.where(lane >= first + GROUP, done[:, :half], 0.0)
        high, mid, low3 = parts(done)
        high_l, mid_l, low_l = parts(later)
        lhs = jnp.concatenate([high_l, high_l, mid_l, high_l, low_l, mid_l], axis=0).T
        rhs = jnp.concatenate([high, mid, high, low3, high, mid], axis=0)
        aug[start:, :] -= lax.dot_general(
            lhs[start:], rhs, (((1,), (0,)), ((), ())),
            precision=lax.Precision.DEFAULT, preferred_element_type=jnp.float32,
        )
        aug[pl.ds(first, GROUP), :] = done
        return carry

    steps = half // GROUP
    lax.fori_loop(0, steps // 2, functools.partial(step, 0), 0)
    lax.fori_loop(steps // 2, steps, functools.partial(step, half // 2), 0)


def factor_panel(block, aug, factor, inverse, width):
    half = width // 2
    row = lax.broadcasted_iota(jnp.int32, (half, half), 0)
    col = lax.broadcasted_iota(jnp.int32, (half, half), 1)
    eye = jnp.where(row == col, 1.0, 0.0).astype(jnp.float32)
    zero = jnp.zeros((half, half), jnp.float32)

    def diagonal(value):
        aug[:, :half] = value
        aug[:, half:] = eye
        eliminate(aug, half)
        return jnp.where(row <= col, aug[:, :half], 0.0).T, aug[:, half:]

    low1, inv1 = diagonal(block[:half, :half])
    factor[:half, :half] = low1
    inverse[:half, :half] = inv1
    factor[:half, half:] = zero
    inverse[:half, half:] = zero
    below = matmul_t(block[half:, :half], inv1)
    factor[half:, :half] = below
    low2, inv2 = diagonal(block[half:, half:] - matmul_t(below, below))
    factor[half:, half:] = low2
    inverse[half:, half:] = inv2
    inverse[half:, :half] = -matmul(inv2, matmul(below, inverse[:half, :half]))


def kernel(
    sizes, window, out, diag, across, panel, share, staged, aug, factor, inverse, cross, rest, left,
    diag_send, diag_recv, pass_send, pass_recv, across_send, across_recv, panel_send, panel_recv, local_sem, share_sem, out_sem,
):
    layers, grid_rows, grid_cols, row_blocks, col_blocks, width = sizes
    rows_here = width // layers
    me_layer, me_row, me_col = lax.axis_index("layer"), lax.axis_index("row"), lax.axis_index("col")

    def at(layer, row, col):
        return (lax.rem(me_layer + layer, layers), lax.rem(me_row + row, grid_rows), lax.rem(me_col + col, grid_cols))

    def remote(src, dst, send, recv, target):
        return pltpu.make_async_remote_copy(
            src_ref=src, dst_ref=dst, send_sem=send, recv_sem=recv, device_id=target,
            device_id_type=pl.DeviceIdType.MESH,
        )

    def stripe(layer):
        return pl.ds(pl.multiple_of(layer * rows_here, rows_here), rows_here)

    here = stripe(me_layer)

    def share_copy(slot):
        return pltpu.make_async_copy(window.at[:, 0, here, slot, 0, :], share.at[slot], share_sem.at[slot])

    grid_peers = [(row, col) for row in range(grid_rows) for col in range(grid_cols) if row or col]
    barrier = pltpu.get_barrier_semaphore()
    for row, col in grid_peers:
        pl.semaphore_signal(barrier, inc=1, device_id=at(0, row, col), device_id_type=pl.DeviceIdType.MESH)
    for layer in range(1, layers):
        pl.semaphore_signal(barrier, inc=1, device_id=at(layer, 0, 0), device_id_type=pl.DeviceIdType.MESH)
    for slot in range(col_blocks):
        share_copy(slot).start()
    pl.semaphore_wait(barrier, len(grid_peers) + layers - 1)

    diag_src = window.at[0, 0, here, 0, 0, :]

    def diag_copy(b, n):
        return remote(diag_src, diag.at[b, here, :], diag_send.at[b, n], diag_recv.at[b], at(0, *grid_peers[n]))

    def diag_local(b):
        return pltpu.make_async_copy(diag_src, diag.at[b, here, :], local_sem.at[b])

    def pass_copy(b, n):
        part = diag.at[b, here, :]
        return remote(part, part, pass_send.at[b, n - 1], pass_recv.at[b, n - 1], at(n, 0, 0))

    def across_copy(k, slot, n):
        return remote(
            window.at[0, 0, :, slot, 0, :], across.at[k, slot], across_send.at[k, slot, n - 1],
            across_recv.at[k, slot], at(0, n, 0),
        )

    def across_local(k, slot):
        return pltpu.make_async_copy(window.at[0, 0, :, slot, 0, :], across.at[k, slot], across_recv.at[k, slot])

    panel_src = window.at[:, 0, here, 0, 0, :]

    def panel_copy(k, n):
        return remote(panel_src, panel.at[k], panel_send.at[k, n - 1], panel_recv.at[k], at(0, 0, n))

    def panel_local(k):
        return pltpu.make_async_copy(panel_src, panel.at[k], panel_recv.at[k])

    owners = [(me_row == i) & (me_col == j) for i, j in BLOCKS]
    for b in range(len(BLOCKS)):

        @pl.when(owners[b])
        def _(b=b):
            for n in range(len(grid_peers)):
                diag_copy(b, n).start()
            diag_local(b).start()

    for k in range(PANELS):

        @pl.when(me_col == k)
        def _(k=k):
            for n in range(1, grid_cols):
                panel_copy(k, n).start()
            panel_local(k).start()

        @pl.when(me_row == k)
        def _(k=k):
            for slot in range(col_blocks):
                for n in range(1, grid_rows):
                    across_copy(k, slot, n).start()
                across_local(k, slot).start()

    for b in range(len(BLOCKS)):

        @pl.when(owners[b])
        def _(b=b):
            diag_local(b).wait()

        @pl.when(jnp.logical_not(owners[b]))
        def _(b=b):
            diag_copy(b, 0).wait_recv()

        for n in range(1, layers):
            pass_copy(b, n).start()

    def diag_arrived(b):
        for n in range(1, layers):
            pass_copy(b, n).wait_recv()

    diag_arrived(0)
    factor_panel(diag.at[0], aug, factor.at[0], inverse.at[0], width)
    diag_arrived(1)
    cross[...] = matmul_t(diag[1], inverse[0])
    diag_arrived(2)
    rest[...] = diag[2] - matmul_t(cross[...], cross[...])
    factor_panel(rest, aug, factor.at[1], inverse.at[1], width)

    def panel_arrived(k):
        @pl.when(me_col == k)
        def _():
            panel_local(k).wait()

        @pl.when(me_col != k)
        def _():
            panel_copy(k, 1).wait_recv()

    def across_arrived(k, slot):
        @pl.when(me_row == k)
        def _():
            across_local(k, slot).wait()

        @pl.when(me_row != k)
        def _():
            across_copy(k, slot, 1).wait_recv()

    total = row_blocks * rows_here
    for k in range(PANELS):
        panel_arrived(k)
    left[0] = matmul_t(panel[0].reshape(total, width), inverse[0])
    left[1] = matmul_t(panel[1].reshape(total, width) - matmul_t(left[0], cross[...]), inverse[1])
    first0 = jnp.where(me_row == 0, factor[0, here, :], left[0, :rows_here, :])
    first1 = jnp.where(me_row == 0, 0.0, jnp.where(me_row == 1, factor[1, here, :], left[1, :rows_here, :]))

    def out_copy(slot):
        return pltpu.make_async_copy(staged.at[slot], out.at[:, 0, :, slot, 0, :], out_sem.at[slot])

    for slot in range(col_blocks):
        for k in range(PANELS):
            across_arrived(k, slot)
        share_copy(slot).wait()
        right0 = matmul(inverse[0], across[0, slot])
        right1 = matmul(inverse[1], across[1, slot] - matmul(cross[...], right0))
        updated = share[slot].reshape(total, width) - matmul(left[0], right0) - matmul(left[1], right1)
        number = slot * grid_cols + me_col
        value = jnp.where(number == 0, left[0], jnp.where(number == 1, left[1], updated))
        staged[slot] = value.reshape(row_blocks, rows_here, width)
        plain = jnp.where(me_row < PANELS, 0.0, updated[:rows_here])
        staged[slot, 0] = jnp.where(number == 0, first0, jnp.where(number == 1, first1, plain))
        out_copy(slot).start()

    for b in range(len(BLOCKS)):

        @pl.when(owners[b])
        def _(b=b):
            for n in range(len(grid_peers)):
                diag_copy(b, n).wait_send()

        for n in range(1, layers):
            pass_copy(b, n).wait_send()
    for k in range(PANELS):

        @pl.when(me_col == k)
        def _(k=k):
            for n in range(1, grid_cols):
                panel_copy(k, n).wait_send()

        @pl.when(me_row == k)
        def _(k=k):
            for slot in range(col_blocks):
                for n in range(1, grid_rows):
                    across_copy(k, slot, n).wait_send()
    for slot in range(col_blocks):
        out_copy(slot).wait()


def local(sizes, schur_window):
    layers, grid_rows, grid_cols, row_blocks, col_blocks, width = sizes
    rows_here = width // layers
    anywhere = pl.BlockSpec(memory_space=pl.ANY)
    dma = pltpu.SemaphoreType.DMA
    diagonals, peers, half = len(BLOCKS), grid_rows * grid_cols - 1, width // 2
    f32 = jnp.float32
    return pl.pallas_call(
        functools.partial(kernel, sizes),
        out_shape=jax.ShapeDtypeStruct((row_blocks, 1, rows_here, col_blocks, 1, width), f32),
        in_specs=[anywhere],
        out_specs=anywhere,
        scratch_shapes=[
            pltpu.VMEM((diagonals, width, width), f32),
            pltpu.VMEM((PANELS, col_blocks, width, width), f32),
            pltpu.VMEM((PANELS, row_blocks, rows_here, width), f32),
            pltpu.VMEM((col_blocks, row_blocks, rows_here, width), f32),
            pltpu.VMEM((col_blocks, row_blocks, rows_here, width), f32),
            pltpu.VMEM((half, width), f32),
            pltpu.VMEM((PANELS, width, width), f32),
            pltpu.VMEM((PANELS, width, width), f32),
            pltpu.VMEM((width, width), f32),
            pltpu.VMEM((width, width), f32),
            pltpu.VMEM((PANELS, row_blocks * rows_here, width), f32),
            dma((diagonals, peers)),
            dma((diagonals,)),
            dma((diagonals, layers - 1)),
            dma((diagonals, layers - 1)),
            dma((PANELS, col_blocks, grid_rows - 1)),
            dma((PANELS, col_blocks)),
            dma((PANELS, grid_cols - 1)),
            dma((PANELS,)),
            dma((diagonals,)),
            dma((col_blocks,)),
            dma((col_blocks,)),
        ],
        compiler_params=pltpu.CompilerParams(collective_id=0, has_side_effects=True),
        name="window",
    )(schur_window)


def solution(mesh):
    def body(schur_window):
        row_blocks, _, width, col_blocks, _, _ = schur_window.shape
        sizes = (mesh.shape["layer"], mesh.shape["row"], mesh.shape["col"], row_blocks, col_blocks, width)
        return local(sizes, schur_window)

    return jax.shard_map(
        body,
        mesh=mesh,
        in_specs=(P(None, "row", None, None, "col", None),),
        out_specs=P(None, "row", "layer", None, "col", None),
        check_vma=False,
    )
```

```python
import functools

import jax
import jax.numpy as jnp
from jax import lax
from jax.experimental import pallas as pl
from jax.experimental.pallas import tpu as pltpu
from jax.sharding import PartitionSpec as P

PANELS = 2
GROUP = 8
BLOCKS = ((0, 0), (1, 0), (1, 1))


def dot(a, b, lhs, rhs):
    return lax.dot_general(
        a, b, (((lhs,), (rhs,)), ((), ())),
        precision=lax.Precision.HIGHEST, preferred_element_type=jnp.float32,
    )


def matmul(a, b):
    return dot(a, b, 1, 0)


def matmul_t(a, b):
    return dot(a, b, 1, 1)


def update(a, b, rhs):
    a0, b0 = a.astype(jnp.bfloat16), b.astype(jnp.bfloat16)
    a1 = (a - a0.astype(jnp.float32)).astype(jnp.bfloat16)
    b1 = (b - b0.astype(jnp.float32)).astype(jnp.bfloat16)

    def product(x, y):
        return lax.dot_general(x, y, (((1,), (rhs,)), ((), ())), preferred_element_type=jnp.float32)

    return product(a0, b0) + (product(a0, b1) + product(a1, b0))


def parts(value):
    high = value.astype(jnp.bfloat16).astype(jnp.float32)
    mid = (value - high).astype(jnp.bfloat16).astype(jnp.float32)
    return high, mid, value - high - mid


def eliminate(aug, half):
    lane = lax.broadcasted_iota(jnp.int32, (GROUP, half), 1)
    sub = lax.broadcasted_iota(jnp.int32, (GROUP, 2 * half), 0)

    def step(start, s, carry):
        first = pl.multiple_of(s * GROUP, GROUP)
        block = aug[pl.ds(first, GROUP), :]
        turned = pltpu.roll(block[:, :half], lax.rem(half - first, half), 1)
        rows = [jnp.broadcast_to(block[j : j + 1, :], (GROUP, 2 * half)) for j in range(GROUP)]
        entry = [
            [jnp.broadcast_to(turned[j : j + 1, k : k + 1], (GROUP, half)) if k >= j else None for k in range(GROUP)]
            for j in range(GROUP)
        ]
        done = jnp.zeros((GROUP, 2 * half), jnp.float32)
        for j in range(GROUP):
            scale = lax.rsqrt(entry[j][j])
            row = rows[j] * jnp.concatenate([scale, scale], axis=1)
            done = jnp.where(sub == j, row, done)
            low = [entry[j][k] * scale if k > j else None for k in range(GROUP)]
            for k in range(j + 1, GROUP):
                for m in range(k, GROUP):
                    entry[k][m] = entry[k][m] - low[k] * low[m]
                rows[k] = rows[k] - jnp.concatenate([low[k], low[k]], axis=1) * row
        later = jnp.where(lane >= first + GROUP, done[:, :half], 0.0)
        high, mid, low3 = parts(done)
        high_l, mid_l, low_l = parts(later)
        lhs = jnp.concatenate([high_l, high_l, mid_l, high_l, low_l, mid_l], axis=0).T
        rhs = jnp.concatenate([high, mid, high, low3, high, mid], axis=0)
        aug[start:, :] -= lax.dot_general(
            lhs[start:], rhs, (((1,), (0,)), ((), ())),
            precision=lax.Precision.DEFAULT, preferred_element_type=jnp.float32,
        )
        aug[pl.ds(first, GROUP), :] = done
        return carry

    steps = half // GROUP
    lax.fori_loop(0, steps // 2, functools.partial(step, 0), 0)
    lax.fori_loop(steps // 2, steps, functools.partial(step, half // 2), 0)


def factor_panel(block, aug, factor, inverse, width, between):
    half = width // 2
    row = lax.broadcasted_iota(jnp.int32, (half, half), 0)
    col = lax.broadcasted_iota(jnp.int32, (half, half), 1)
    eye = jnp.where(row == col, 1.0, 0.0).astype(jnp.float32)
    zero = jnp.zeros((half, half), jnp.float32)

    def diagonal(value):
        aug[:, :half] = value
        aug[:, half:] = eye
        eliminate(aug, half)
        return jnp.where(row <= col, aug[:, :half], 0.0).T, aug[:, half:]

    low1, inv1 = diagonal(block[:half, :half])
    if between is not None:
        between()
    factor[:half, :half] = low1
    inverse[:half, :half] = inv1
    factor[:half, half:] = zero
    inverse[:half, half:] = zero
    below = matmul_t(block[half:, :half], inv1)
    factor[half:, :half] = below
    low2, inv2 = diagonal(block[half:, half:] - matmul_t(below, below))
    factor[half:, half:] = low2
    inverse[half:, half:] = inv2
    inverse[half:, :half] = -matmul(inv2, matmul(below, inverse[:half, :half]))


def kernel(
    sizes, window, out, diag, across, panel, share, staged, aug, factor, inverse, cross, rest, left,
    diag_send, diag_recv, pass_send, pass_recv, across_send, across_recv, panel_send, panel_recv, local_sem, share_sem, out_sem,
):
    layers, grid_rows, grid_cols, row_blocks, col_blocks, width = sizes
    rows_here = width // layers
    me_layer, me_row, me_col = lax.axis_index("layer"), lax.axis_index("row"), lax.axis_index("col")

    def at(layer, row, col):
        return (lax.rem(me_layer + layer, layers), lax.rem(me_row + row, grid_rows), lax.rem(me_col + col, grid_cols))

    def remote(src, dst, send, recv, target):
        return pltpu.make_async_remote_copy(
            src_ref=src, dst_ref=dst, send_sem=send, recv_sem=recv, device_id=target,
            device_id_type=pl.DeviceIdType.MESH,
        )

    def stripe(layer):
        return pl.ds(pl.multiple_of(layer * rows_here, rows_here), rows_here)

    here = stripe(me_layer)

    def share_copy(slot):
        return pltpu.make_async_copy(window.at[:, 0, here, slot, 0, :], share.at[slot], share_sem.at[slot])

    grid_peers = [(row, col) for row in range(grid_rows) for col in range(grid_cols) if row or col]
    barrier = pltpu.get_barrier_semaphore()
    for row, col in grid_peers:
        pl.semaphore_signal(barrier, inc=1, device_id=at(0, row, col), device_id_type=pl.DeviceIdType.MESH)
    for layer in range(1, layers):
        pl.semaphore_signal(barrier, inc=1, device_id=at(layer, 0, 0), device_id_type=pl.DeviceIdType.MESH)
    for slot in range(col_blocks):
        share_copy(slot).start()
    pl.semaphore_wait(barrier, len(grid_peers) + layers - 1)

    diag_src = window.at[0, 0, here, 0, 0, :]

    def diag_copy(b, n):
        return remote(diag_src, diag.at[b, here, :], diag_send.at[b, n], diag_recv.at[b], at(0, *grid_peers[n]))

    def diag_local(b):
        return pltpu.make_async_copy(diag_src, diag.at[b, here, :], local_sem.at[b])

    def pass_copy(b, n):
        part = diag.at[b, here, :]
        return remote(part, part, pass_send.at[b, n - 1], pass_recv.at[b, n - 1], at(n, 0, 0))

    def across_copy(k, slot, n):
        return remote(
            window.at[0, 0, :, slot, 0, :], across.at[k, slot], across_send.at[k, slot, n - 1],
            across_recv.at[k, slot], at(0, n, 0),
        )

    def across_local(k, slot):
        return pltpu.make_async_copy(window.at[0, 0, :, slot, 0, :], across.at[k, slot], across_recv.at[k, slot])

    panel_src = window.at[:, 0, here, 0, 0, :]

    def panel_copy(k, n):
        return remote(panel_src, panel.at[k], panel_send.at[k, n - 1], panel_recv.at[k], at(0, 0, n))

    def panel_local(k):
        return pltpu.make_async_copy(panel_src, panel.at[k], panel_recv.at[k])

    owners = [(me_row == i) & (me_col == j) for i, j in BLOCKS]
    def diag_send_out(b):
        @pl.when(owners[b])
        def _():
            for n in range(len(grid_peers)):
                diag_copy(b, n).start()
            diag_local(b).start()

    def diag_pass_on(b):
        @pl.when(owners[b])
        def _():
            diag_local(b).wait()

        @pl.when(jnp.logical_not(owners[b]))
        def _():
            diag_copy(b, 0).wait_recv()

        for n in range(1, layers):
            pass_copy(b, n).start()

    def pass_later():
        for b in range(1, len(BLOCKS)):
            diag_pass_on(b)

    diag_send_out(0)
    diag_pass_on(0)
    for b in range(1, len(BLOCKS)):
        diag_send_out(b)
    for k in range(PANELS):

        @pl.when(me_row == k)
        def _(k=k):
            for slot in range(col_blocks):
                for n in range(1, grid_rows):
                    across_copy(k, slot, n).start()
                across_local(k, slot).start()

        @pl.when(me_col == k)
        def _(k=k):
            for n in range(1, grid_cols):
                panel_copy(k, n).start()
            panel_local(k).start()

    def diag_arrived(b):
        for n in range(1, layers):
            pass_copy(b, n).wait_recv()

    diag_arrived(0)
    factor_panel(diag.at[0], aug, factor.at[0], inverse.at[0], width, pass_later)
    diag_arrived(1)
    cross[...] = matmul_t(diag[1], inverse[0])
    diag_arrived(2)
    rest[...] = diag[2] - matmul_t(cross[...], cross[...])
    factor_panel(rest, aug, factor.at[1], inverse.at[1], width, None)

    def panel_arrived(k):
        @pl.when(me_col == k)
        def _():
            panel_local(k).wait()

        @pl.when(me_col != k)
        def _():
            panel_copy(k, 1).wait_recv()

    def across_arrived(k, slot):
        @pl.when(me_row == k)
        def _():
            across_local(k, slot).wait()

        @pl.when(me_row != k)
        def _():
            across_copy(k, slot, 1).wait_recv()

    total = row_blocks * rows_here
    skipped = rows_here if grid_rows <= PANELS else 0
    for k in range(PANELS):
        panel_arrived(k)
    left[0] = matmul_t(panel[0].reshape(total, width), inverse[0])
    left[1] = matmul_t(panel[1].reshape(total, width) - update(left[0], cross[...], 1), inverse[1])
    first0 = jnp.where(me_row == 0, factor[0, here, :], left[0, :rows_here, :])
    first1 = jnp.where(me_row == 0, 0.0, jnp.where(me_row == 1, factor[1, here, :], left[1, :rows_here, :]))

    def out_copy(slot):
        return pltpu.make_async_copy(staged.at[slot], out.at[:, 0, :, slot, 0, :], out_sem.at[slot])

    for slot in range(col_blocks):
        for k in range(PANELS):
            across_arrived(k, slot)
        share_copy(slot).wait()
        right0 = matmul(inverse[0], across[0, slot])
        right1 = matmul(inverse[1], across[1, slot] - update(cross[...], right0, 0))
        number = slot * grid_cols + me_col
        rest_rows = total - skipped
        updated = share[slot].reshape(total, width)[skipped:]
        updated -= update(left[0, skipped:, :], right0, 0) + update(left[1, skipped:, :], right1, 0)
        value = jnp.where(number == 0, left[0, skipped:, :], jnp.where(number == 1, left[1, skipped:, :], updated))
        staged[slot, skipped // rows_here :] = value.reshape(rest_rows // rows_here, rows_here, width)
        plain = 0.0 if skipped else jnp.where(me_row < PANELS, 0.0, updated[:rows_here])
        staged[slot, 0] = jnp.where(number == 0, first0, jnp.where(number == 1, first1, plain))
        out_copy(slot).start()

    for b in range(len(BLOCKS)):

        @pl.when(owners[b])
        def _(b=b):
            for n in range(len(grid_peers)):
                diag_copy(b, n).wait_send()

        for n in range(1, layers):
            pass_copy(b, n).wait_send()
    for k in range(PANELS):

        @pl.when(me_col == k)
        def _(k=k):
            for n in range(1, grid_cols):
                panel_copy(k, n).wait_send()

        @pl.when(me_row == k)
        def _(k=k):
            for slot in range(col_blocks):
                for n in range(1, grid_rows):
                    across_copy(k, slot, n).wait_send()
    for slot in range(col_blocks):
        out_copy(slot).wait()


def local(sizes, schur_window):
    layers, grid_rows, grid_cols, row_blocks, col_blocks, width = sizes
    rows_here = width // layers
    anywhere = pl.BlockSpec(memory_space=pl.ANY)
    dma = pltpu.SemaphoreType.DMA
    diagonals, peers, half = len(BLOCKS), grid_rows * grid_cols - 1, width // 2
    f32 = jnp.float32
    return pl.pallas_call(
        functools.partial(kernel, sizes),
        out_shape=jax.ShapeDtypeStruct((row_blocks, 1, rows_here, col_blocks, 1, width), f32),
        in_specs=[anywhere],
        out_specs=anywhere,
        scratch_shapes=[
            pltpu.VMEM((diagonals, width, width), f32),
            pltpu.VMEM((PANELS, col_blocks, width, width), f32),
            pltpu.VMEM((PANELS, row_blocks, rows_here, width), f32),
            pltpu.VMEM((col_blocks, row_blocks, rows_here, width), f32),
            pltpu.VMEM((col_blocks, row_blocks, rows_here, width), f32),
            pltpu.VMEM((half, width), f32),
            pltpu.VMEM((PANELS, width, width), f32),
            pltpu.VMEM((PANELS, width, width), f32),
            pltpu.VMEM((width, width), f32),
            pltpu.VMEM((width, width), f32),
            pltpu.VMEM((PANELS, row_blocks * rows_here, width), f32),
            dma((diagonals, peers)),
            dma((diagonals,)),
            dma((diagonals, layers - 1)),
            dma((diagonals, layers - 1)),
            dma((PANELS, col_blocks, grid_rows - 1)),
            dma((PANELS, col_blocks)),
            dma((PANELS, grid_cols - 1)),
            dma((PANELS,)),
            dma((diagonals,)),
            dma((col_blocks,)),
            dma((col_blocks,)),
        ],
        compiler_params=pltpu.CompilerParams(collective_id=0, has_side_effects=True),
        name="window",
    )(schur_window)


def solution(mesh):
    def body(schur_window):
        row_blocks, _, width, col_blocks, _, _ = schur_window.shape
        sizes = (mesh.shape["layer"], mesh.shape["row"], mesh.shape["col"], row_blocks, col_blocks, width)
        return local(sizes, schur_window)

    return jax.shard_map(
        body,
        mesh=mesh,
        in_specs=(P(None, "row", None, None, "col", None),),
        out_specs=P(None, "row", "layer", None, "col", None),
        check_vma=False,
    )
```

```python
import functools

import jax
import jax.numpy as jnp
from jax import lax
from jax.experimental import pallas as pl
from jax.experimental.pallas import tpu as pltpu
from jax.sharding import PartitionSpec as P

PANELS = 2
GROUP = 8
BLOCKS = ((0, 0, 0, 0), (0, 0, 0, 1), (1, 0, 1, None), (1, 1, 2, None))


def dot(a, b, lhs, rhs):
    return lax.dot_general(
        a, b, (((lhs,), (rhs,)), ((), ())),
        precision=lax.Precision.HIGHEST, preferred_element_type=jnp.float32,
    )


def matmul(a, b):
    return dot(a, b, 1, 0)


def matmul_t(a, b):
    return dot(a, b, 1, 1)


def update(a, b, rhs):
    a0, b0 = a.astype(jnp.bfloat16), b.astype(jnp.bfloat16)
    a1 = (a - a0.astype(jnp.float32)).astype(jnp.bfloat16)
    b1 = (b - b0.astype(jnp.float32)).astype(jnp.bfloat16)

    def product(x, y):
        return lax.dot_general(x, y, (((1,), (rhs,)), ((), ())), preferred_element_type=jnp.float32)

    return product(a0, b0) + (product(a0, b1) + product(a1, b0))


def parts(value):
    high = value.astype(jnp.bfloat16).astype(jnp.float32)
    mid = (value - high).astype(jnp.bfloat16).astype(jnp.float32)
    return high, mid, value - high - mid


def eliminate(aug, half, midway):
    lane = lax.broadcasted_iota(jnp.int32, (GROUP, half), 1)
    sub = lax.broadcasted_iota(jnp.int32, (GROUP, 2 * half), 0)

    def step(start, s, carry):
        first = pl.multiple_of(s * GROUP, GROUP)
        block = aug[pl.ds(first, GROUP), :]
        turned = pltpu.roll(block[:, :half], lax.rem(half - first, half), 1)
        rows = [jnp.broadcast_to(block[j : j + 1, :], (GROUP, 2 * half)) for j in range(GROUP)]
        entry = [
            [jnp.broadcast_to(turned[j : j + 1, k : k + 1], (GROUP, half)) if k >= j else None for k in range(GROUP)]
            for j in range(GROUP)
        ]
        done = jnp.zeros((GROUP, 2 * half), jnp.float32)
        for j in range(GROUP):
            scale = lax.rsqrt(entry[j][j])
            row = rows[j] * jnp.concatenate([scale, scale], axis=1)
            done = jnp.where(sub == j, row, done)
            low = [entry[j][k] * scale if k > j else None for k in range(GROUP)]
            for k in range(j + 1, GROUP):
                for m in range(k, GROUP):
                    entry[k][m] = entry[k][m] - low[k] * low[m]
                rows[k] = rows[k] - jnp.concatenate([low[k], low[k]], axis=1) * row
        later = jnp.where(lane >= first + GROUP, done[:, :half], 0.0)
        high, mid, low3 = parts(done)
        high_l, mid_l, low_l = parts(later)
        lhs = jnp.concatenate([high_l, high_l, mid_l, high_l, low_l, mid_l], axis=0).T
        rhs = jnp.concatenate([high, mid, high, low3, high, mid], axis=0)
        aug[start:, :] -= lax.dot_general(
            lhs[start:], rhs, (((1,), (0,)), ((), ())),
            precision=lax.Precision.DEFAULT, preferred_element_type=jnp.float32,
        )
        aug[pl.ds(first, GROUP), :] = done
        return carry

    steps = half // GROUP
    lax.fori_loop(0, steps // 2, functools.partial(step, 0), 0)
    if midway is not None:
        midway()
    lax.fori_loop(steps // 2, steps, functools.partial(step, half // 2), 0)


def factor_panel(block, aug, factor, inverse, width, midway, between):
    half = width // 2
    row = lax.broadcasted_iota(jnp.int32, (half, half), 0)
    col = lax.broadcasted_iota(jnp.int32, (half, half), 1)
    eye = jnp.where(row == col, 1.0, 0.0).astype(jnp.float32)
    zero = jnp.zeros((half, half), jnp.float32)

    def diagonal(value, midway):
        aug[:, :half] = value
        aug[:, half:] = eye
        eliminate(aug, half, midway)
        return jnp.where(row <= col, aug[:, :half], 0.0).T, aug[:, half:]

    low1, inv1 = diagonal(block[:half, :half], midway)
    if between is not None:
        between()
    factor[:half, :half] = low1
    inverse[:half, :half] = inv1
    factor[:half, half:] = zero
    inverse[:half, half:] = zero
    below = matmul_t(block[half:, :half], inv1)
    factor[half:, :half] = below
    low2, inv2 = diagonal(block[half:, half:] - matmul_t(below, below), None)
    factor[half:, half:] = low2
    inverse[half:, half:] = inv2
    inverse[half:, :half] = -matmul(inv2, matmul(below, inverse[:half, :half]))


def kernel(
    sizes, window, out, diag, across, panel, share, staged, aug, factor, inverse, cross, rest, left,
    diag_send, diag_recv, pass_send, pass_recv, across_send, across_recv, panel_send, panel_recv, local_sem, share_sem, out_sem,
):
    layers, grid_rows, grid_cols, row_blocks, col_blocks, width = sizes
    rows_here = width // layers
    me_layer, me_row, me_col = lax.axis_index("layer"), lax.axis_index("row"), lax.axis_index("col")

    def at(layer, row, col):
        return (lax.rem(me_layer + layer, layers), lax.rem(me_row + row, grid_rows), lax.rem(me_col + col, grid_cols))

    def remote(src, dst, send, recv, target):
        return pltpu.make_async_remote_copy(
            src_ref=src, dst_ref=dst, send_sem=send, recv_sem=recv, device_id=target,
            device_id_type=pl.DeviceIdType.MESH,
        )

    def stripe(layer):
        return pl.ds(pl.multiple_of(layer * rows_here, rows_here), rows_here)

    here = stripe(me_layer)

    def share_copy(slot):
        return pltpu.make_async_copy(window.at[:, 0, here, slot, 0, :], share.at[slot], share_sem.at[slot])

    grid_peers = [(row, col) for row in range(grid_rows) for col in range(grid_cols) if row or col]
    barrier = pltpu.get_barrier_semaphore()
    for row, col in grid_peers:
        pl.semaphore_signal(barrier, inc=1, device_id=at(0, row, col), device_id_type=pl.DeviceIdType.MESH)
    for layer in range(1, layers):
        pl.semaphore_signal(barrier, inc=1, device_id=at(layer, 0, 0), device_id_type=pl.DeviceIdType.MESH)
    for slot in range(col_blocks):
        share_copy(slot).start()
    pl.semaphore_wait(barrier, len(grid_peers) + layers - 1)

    def columns(b):
        side = BLOCKS[b][3]
        return pl.ds(0, width) if side is None else pl.ds(side * (width // 2), width // 2)

    def diag_src(b):
        return window.at[0, 0, here, 0, 0, columns(b)]

    def diag_dst(b):
        return diag.at[BLOCKS[b][2], here, columns(b)]

    def diag_copy(b, n):
        return remote(diag_src(b), diag_dst(b), diag_send.at[b, n], diag_recv.at[b], at(0, *grid_peers[n]))

    def diag_local(b):
        return pltpu.make_async_copy(diag_src(b), diag_dst(b), local_sem.at[b])

    def pass_copy(b, n):
        part = diag_dst(b)
        return remote(part, part, pass_send.at[b, n - 1], pass_recv.at[b, n - 1], at(n, 0, 0))

    def across_copy(k, slot, n):
        return remote(
            window.at[0, 0, :, slot, 0, :], across.at[k, slot], across_send.at[k, slot, n - 1],
            across_recv.at[k, slot], at(0, n, 0),
        )

    def across_local(k, slot):
        return pltpu.make_async_copy(window.at[0, 0, :, slot, 0, :], across.at[k, slot], across_recv.at[k, slot])

    panel_src = window.at[:, 0, here, 0, 0, :]

    def panel_copy(k, n):
        return remote(panel_src, panel.at[k], panel_send.at[k, n - 1], panel_recv.at[k], at(0, 0, n))

    def panel_local(k):
        return pltpu.make_async_copy(panel_src, panel.at[k], panel_recv.at[k])

    owners = [(me_row == i) & (me_col == j) for i, j, _, _ in BLOCKS]
    def diag_send_out(b):
        @pl.when(owners[b])
        def _():
            for n in range(len(grid_peers)):
                diag_copy(b, n).start()
            diag_local(b).start()

    def diag_pass_on(b):
        @pl.when(owners[b])
        def _():
            diag_local(b).wait()

        @pl.when(jnp.logical_not(owners[b]))
        def _():
            diag_copy(b, 0).wait_recv()

        for n in range(1, layers):
            pass_copy(b, n).start()

    def midway():
        diag_pass_on(1)

    def between():
        for b in range(2, len(BLOCKS)):
            diag_pass_on(b)
        diag_arrived(1)

    diag_send_out(0)
    diag_pass_on(0)
    for b in range(1, len(BLOCKS)):
        diag_send_out(b)
    for k in range(PANELS):

        @pl.when(me_row == k)
        def _(k=k):
            for slot in range(col_blocks):
                for n in range(1, grid_rows):
                    across_copy(k, slot, n).start()
                across_local(k, slot).start()

        @pl.when(me_col == k)
        def _(k=k):
            for n in range(1, grid_cols):
                panel_copy(k, n).start()
            panel_local(k).start()

    def diag_arrived(b):
        for n in range(1, layers):
            pass_copy(b, n).wait_recv()

    diag_arrived(0)
    factor_panel(diag.at[0], aug, factor.at[0], inverse.at[0], width, midway, between)
    diag_arrived(2)
    cross[...] = matmul_t(diag[1], inverse[0])
    diag_arrived(3)
    rest[...] = diag[2] - matmul_t(cross[...], cross[...])
    factor_panel(rest, aug, factor.at[1], inverse.at[1], width, None, None)

    def panel_arrived(k):
        @pl.when(me_col == k)
        def _():
            panel_local(k).wait()

        @pl.when(me_col != k)
        def _():
            panel_copy(k, 1).wait_recv()

    def across_arrived(k, slot):
        @pl.when(me_row == k)
        def _():
            across_local(k, slot).wait()

        @pl.when(me_row != k)
        def _():
            across_copy(k, slot, 1).wait_recv()

    total = row_blocks * rows_here
    skipped = rows_here if grid_rows <= PANELS else 0
    for k in range(PANELS):
        panel_arrived(k)
    left[0] = matmul_t(panel[0].reshape(total, width), inverse[0])
    left[1] = matmul_t(panel[1].reshape(total, width) - update(left[0], cross[...], 1), inverse[1])
    first0 = jnp.where(me_row == 0, factor[0, here, :], left[0, :rows_here, :])
    first1 = jnp.where(me_row == 0, 0.0, jnp.where(me_row == 1, factor[1, here, :], left[1, :rows_here, :]))

    def out_copy(slot):
        return pltpu.make_async_copy(staged.at[slot], out.at[:, 0, :, slot, 0, :], out_sem.at[slot])

    for slot in range(col_blocks):
        for k in range(PANELS):
            across_arrived(k, slot)
        share_copy(slot).wait()
        right0 = matmul(inverse[0], across[0, slot])
        right1 = matmul(inverse[1], across[1, slot] - update(cross[...], right0, 0))
        number = slot * grid_cols + me_col
        rest_rows = total - skipped
        updated = share[slot].reshape(total, width)[skipped:]
        updated -= update(left[0, skipped:, :], right0, 0) + update(left[1, skipped:, :], right1, 0)
        value = jnp.where(number == 0, left[0, skipped:, :], jnp.where(number == 1, left[1, skipped:, :], updated))
        staged[slot, skipped // rows_here :] = value.reshape(rest_rows // rows_here, rows_here, width)
        plain = 0.0 if skipped else jnp.where(me_row < PANELS, 0.0, updated[:rows_here])
        staged[slot, 0] = jnp.where(number == 0, first0, jnp.where(number == 1, first1, plain))
        out_copy(slot).start()

    for b in range(len(BLOCKS)):

        @pl.when(owners[b])
        def _(b=b):
            for n in range(len(grid_peers)):
                diag_copy(b, n).wait_send()

        for n in range(1, layers):
            pass_copy(b, n).wait_send()
    for k in range(PANELS):

        @pl.when(me_col == k)
        def _(k=k):
            for n in range(1, grid_cols):
                panel_copy(k, n).wait_send()

        @pl.when(me_row == k)
        def _(k=k):
            for slot in range(col_blocks):
                for n in range(1, grid_rows):
                    across_copy(k, slot, n).wait_send()
    for slot in range(col_blocks):
        out_copy(slot).wait()


def local(sizes, schur_window):
    layers, grid_rows, grid_cols, row_blocks, col_blocks, width = sizes
    rows_here = width // layers
    anywhere = pl.BlockSpec(memory_space=pl.ANY)
    dma = pltpu.SemaphoreType.DMA
    sends, diagonals, peers, half = len(BLOCKS), len({b[2] for b in BLOCKS}), grid_rows * grid_cols - 1, width // 2
    f32 = jnp.float32
    return pl.pallas_call(
        functools.partial(kernel, sizes),
        out_shape=jax.ShapeDtypeStruct((row_blocks, 1, rows_here, col_blocks, 1, width), f32),
        in_specs=[anywhere],
        out_specs=anywhere,
        scratch_shapes=[
            pltpu.VMEM((diagonals, width, width), f32),
            pltpu.VMEM((PANELS, col_blocks, width, width), f32),
            pltpu.VMEM((PANELS, row_blocks, rows_here, width), f32),
            pltpu.VMEM((col_blocks, row_blocks, rows_here, width), f32),
            pltpu.VMEM((col_blocks, row_blocks, rows_here, width), f32),
            pltpu.VMEM((half, width), f32),
            pltpu.VMEM((PANELS, width, width), f32),
            pltpu.VMEM((PANELS, width, width), f32),
            pltpu.VMEM((width, width), f32),
            pltpu.VMEM((width, width), f32),
            pltpu.VMEM((PANELS, row_blocks * rows_here, width), f32),
            dma((sends, peers)),
            dma((sends,)),
            dma((sends, layers - 1)),
            dma((sends, layers - 1)),
            dma((PANELS, col_blocks, grid_rows - 1)),
            dma((PANELS, col_blocks)),
            dma((PANELS, grid_cols - 1)),
            dma((PANELS,)),
            dma((sends,)),
            dma((col_blocks,)),
            dma((col_blocks,)),
        ],
        compiler_params=pltpu.CompilerParams(collective_id=0, has_side_effects=True),
        name="window",
    )(schur_window)


def solution(mesh):
    def body(schur_window):
        row_blocks, _, width, col_blocks, _, _ = schur_window.shape
        sizes = (mesh.shape["layer"], mesh.shape["row"], mesh.shape["col"], row_blocks, col_blocks, width)
        return local(sizes, schur_window)

    return jax.shard_map(
        body,
        mesh=mesh,
        in_specs=(P(None, "row", None, None, "col", None),),
        out_specs=P(None, "row", "layer", None, "col", None),
        check_vma=False,
    )
```

```python
import functools

import jax
import jax.numpy as jnp
from jax import lax
from jax.experimental import pallas as pl
from jax.experimental.pallas import tpu as pltpu
from jax.sharding import PartitionSpec as P

PANELS = 2
GROUP = 8
BLOCKS = ((0, 0, 0, 0), (0, 0, 0, 1), (1, 0, 1, None), (1, 1, 2, None))


def dot(a, b, lhs, rhs):
    return lax.dot_general(
        a, b, (((lhs,), (rhs,)), ((), ())),
        precision=lax.Precision.HIGHEST, preferred_element_type=jnp.float32,
    )


def matmul(a, b):
    return dot(a, b, 1, 0)


def matmul_t(a, b):
    return dot(a, b, 1, 1)


def update(a, b, rhs):
    a0, b0 = a.astype(jnp.bfloat16), b.astype(jnp.bfloat16)
    a1 = (a - a0.astype(jnp.float32)).astype(jnp.bfloat16)
    b1 = (b - b0.astype(jnp.float32)).astype(jnp.bfloat16)

    def product(x, y):
        return lax.dot_general(x, y, (((1,), (rhs,)), ((), ())), preferred_element_type=jnp.float32)

    return product(a0, b0) + (product(a0, b1) + product(a1, b0))


def parts(value):
    high = value.astype(jnp.bfloat16).astype(jnp.float32)
    mid = (value - high).astype(jnp.bfloat16).astype(jnp.float32)
    return high, mid, value - high - mid


def eliminate(aug, half, midway):
    lane = lax.broadcasted_iota(jnp.int32, (GROUP, half), 1)
    sub = lax.broadcasted_iota(jnp.int32, (GROUP, 2 * half), 0)

    def step(start, s, carry):
        first = pl.multiple_of(s * GROUP, GROUP)
        block = aug[pl.ds(first, GROUP), :]
        turned = pltpu.roll(block[:, :half], lax.rem(half - first, half), 1)
        rows = [jnp.broadcast_to(block[j : j + 1, :], (GROUP, 2 * half)) for j in range(GROUP)]
        entry = [
            [jnp.broadcast_to(turned[j : j + 1, k : k + 1], (GROUP, half)) if k >= j else None for k in range(GROUP)]
            for j in range(GROUP)
        ]
        done = jnp.zeros((GROUP, 2 * half), jnp.float32)
        for j in range(GROUP):
            scale = lax.rsqrt(entry[j][j])
            row = rows[j] * jnp.concatenate([scale, scale], axis=1)
            done = jnp.where(sub == j, row, done)
            low = [entry[j][k] * scale if k > j else None for k in range(GROUP)]
            for k in range(j + 1, GROUP):
                for m in range(k, GROUP):
                    entry[k][m] = entry[k][m] - low[k] * low[m]
                rows[k] = rows[k] - jnp.concatenate([low[k], low[k]], axis=1) * row
        later = jnp.where(lane >= first + GROUP, done[:, :half], 0.0)
        high, mid, low3 = parts(done)
        high_l, mid_l, low_l = parts(later)
        lhs = jnp.concatenate([high_l, high_l, mid_l, high_l, low_l, mid_l], axis=0).T
        rhs = jnp.concatenate([high, mid, high, low3, high, mid], axis=0)
        aug[start:, :] -= lax.dot_general(
            lhs[start:], rhs, (((1,), (0,)), ((), ())),
            precision=lax.Precision.DEFAULT, preferred_element_type=jnp.float32,
        )
        aug[pl.ds(first, GROUP), :] = done
        return carry

    steps = half // GROUP
    lax.fori_loop(0, steps // 2, functools.partial(step, 0), 0)
    if midway is not None:
        midway()
    lax.fori_loop(steps // 2, steps, functools.partial(step, half // 2), 0)


def factor_panel(block, aug, factor, inverse, width, midway, between):
    half = width // 2
    row = lax.broadcasted_iota(jnp.int32, (half, half), 0)
    col = lax.broadcasted_iota(jnp.int32, (half, half), 1)
    eye = jnp.where(row == col, 1.0, 0.0).astype(jnp.float32)
    zero = jnp.zeros((half, half), jnp.float32)

    def diagonal(value, midway):
        aug[:, :half] = value
        aug[:, half:] = eye
        eliminate(aug, half, midway)
        return jnp.where(row <= col, aug[:, :half], 0.0).T, aug[:, half:]

    low1, inv1 = diagonal(block[:half, :half], midway)
    if between is not None:
        between()
    factor[:half, :half] = low1
    inverse[:half, :half] = inv1
    factor[:half, half:] = zero
    inverse[:half, half:] = zero
    below = matmul_t(block[half:, :half], inv1)
    factor[half:, :half] = below
    low2, inv2 = diagonal(block[half:, half:] - matmul_t(below, below), None)
    factor[half:, half:] = low2
    inverse[half:, half:] = inv2
    inverse[half:, :half] = -matmul(inv2, matmul(below, inverse[:half, :half]))


def kernel(
    sizes, window, out, diag, across, panel, share, staged, aug, factor, inverse, cross, rest, left,
    diag_send, diag_recv, pass_send, pass_recv, across_send, across_recv, panel_send, panel_recv, local_sem, share_sem, out_sem,
):
    layers, grid_rows, grid_cols, row_blocks, col_blocks, width = sizes
    rows_here = width // layers
    me_layer, me_row, me_col = lax.axis_index("layer"), lax.axis_index("row"), lax.axis_index("col")

    def at(layer, row, col):
        return (lax.rem(me_layer + layer, layers), lax.rem(me_row + row, grid_rows), lax.rem(me_col + col, grid_cols))

    def remote(src, dst, send, recv, target):
        return pltpu.make_async_remote_copy(
            src_ref=src, dst_ref=dst, send_sem=send, recv_sem=recv, device_id=target,
            device_id_type=pl.DeviceIdType.MESH,
        )

    def stripe(layer):
        return pl.ds(pl.multiple_of(layer * rows_here, rows_here), rows_here)

    here = stripe(me_layer)

    def share_copy(slot):
        return pltpu.make_async_copy(window.at[:, 0, here, slot, 0, :], share.at[slot], share_sem.at[slot])

    grid_peers = [(row, col) for row in range(grid_rows) for col in range(grid_cols) if row or col]
    grid_peers.sort(key=lambda peer: -sum(peer))
    barrier = pltpu.get_barrier_semaphore()
    for row, col in grid_peers:
        pl.semaphore_signal(barrier, inc=1, device_id=at(0, row, col), device_id_type=pl.DeviceIdType.MESH)
    for layer in range(1, layers):
        pl.semaphore_signal(barrier, inc=1, device_id=at(layer, 0, 0), device_id_type=pl.DeviceIdType.MESH)
    for slot in range(col_blocks):
        share_copy(slot).start()
    pl.semaphore_wait(barrier, len(grid_peers) + layers - 1)

    def columns(b):
        side = BLOCKS[b][3]
        return pl.ds(0, width) if side is None else pl.ds(side * (width // 2), width // 2)

    def diag_src(b):
        return window.at[0, 0, here, 0, 0, columns(b)]

    def diag_dst(b):
        return diag.at[BLOCKS[b][2], here, columns(b)]

    def diag_copy(b, n):
        return remote(diag_src(b), diag_dst(b), diag_send.at[b, n], diag_recv.at[b], at(0, *grid_peers[n]))

    def diag_local(b):
        return pltpu.make_async_copy(diag_src(b), diag_dst(b), local_sem.at[b])

    def pass_copy(b, n):
        part = diag_dst(b)
        return remote(part, part, pass_send.at[b, n - 1], pass_recv.at[b, n - 1], at(n, 0, 0))

    def across_copy(k, slot, n):
        return remote(
            window.at[0, 0, :, slot, 0, :], across.at[k, slot], across_send.at[k, slot, n - 1],
            across_recv.at[k, slot], at(0, n, 0),
        )

    def across_local(k, slot):
        return pltpu.make_async_copy(window.at[0, 0, :, slot, 0, :], across.at[k, slot], across_recv.at[k, slot])

    panel_src = window.at[:, 0, here, 0, 0, :]

    def panel_copy(k, n):
        return remote(panel_src, panel.at[k], panel_send.at[k, n - 1], panel_recv.at[k], at(0, 0, n))

    def panel_local(k):
        return pltpu.make_async_copy(panel_src, panel.at[k], panel_recv.at[k])

    owners = [(me_row == i) & (me_col == j) for i, j, _, _ in BLOCKS]
    def diag_send_out(b):
        @pl.when(owners[b])
        def _():
            for n in range(len(grid_peers)):
                diag_copy(b, n).start()
            diag_local(b).start()

    def diag_pass_on(b):
        @pl.when(owners[b])
        def _():
            diag_local(b).wait()

        @pl.when(jnp.logical_not(owners[b]))
        def _():
            diag_copy(b, 0).wait_recv()

        for n in range(1, layers):
            pass_copy(b, n).start()

    def midway():
        diag_pass_on(1)

    def between():
        for b in range(2, len(BLOCKS)):
            diag_pass_on(b)
        diag_arrived(1)

    diag_send_out(0)
    diag_pass_on(0)
    for b in range(1, len(BLOCKS)):
        diag_send_out(b)
    for k in range(PANELS):

        @pl.when(me_row == k)
        def _(k=k):
            for slot in range(col_blocks):
                for n in range(1, grid_rows):
                    across_copy(k, slot, n).start()
                across_local(k, slot).start()

        @pl.when(me_col == k)
        def _(k=k):
            for n in range(1, grid_cols):
                panel_copy(k, n).start()
            panel_local(k).start()

    def diag_arrived(b):
        for n in range(1, layers):
            pass_copy(b, n).wait_recv()

    diag_arrived(0)
    factor_panel(diag.at[0], aug, factor.at[0], inverse.at[0], width, midway, between)
    diag_arrived(2)
    cross[...] = matmul_t(diag[1], inverse[0])
    diag_arrived(3)
    rest[...] = diag[2] - matmul_t(cross[...], cross[...])
    factor_panel(rest, aug, factor.at[1], inverse.at[1], width, None, None)

    def panel_arrived(k):
        @pl.when(me_col == k)
        def _():
            panel_local(k).wait()

        @pl.when(me_col != k)
        def _():
            panel_copy(k, 1).wait_recv()

    def across_arrived(k, slot):
        @pl.when(me_row == k)
        def _():
            across_local(k, slot).wait()

        @pl.when(me_row != k)
        def _():
            across_copy(k, slot, 1).wait_recv()

    total = row_blocks * rows_here
    skipped = rows_here if grid_rows <= PANELS else 0
    for k in range(PANELS):
        panel_arrived(k)
    left[0] = matmul_t(panel[0].reshape(total, width), inverse[0])
    left[1] = matmul_t(panel[1].reshape(total, width) - update(left[0], cross[...], 1), inverse[1])
    first0 = jnp.where(me_row == 0, factor[0, here, :], left[0, :rows_here, :])
    first1 = jnp.where(me_row == 0, 0.0, jnp.where(me_row == 1, factor[1, here, :], left[1, :rows_here, :]))

    def out_copy(slot):
        return pltpu.make_async_copy(staged.at[slot], out.at[:, 0, :, slot, 0, :], out_sem.at[slot])

    for slot in range(col_blocks):
        for k in range(PANELS):
            across_arrived(k, slot)
        share_copy(slot).wait()
        right0 = matmul(inverse[0], across[0, slot])
        right1 = matmul(inverse[1], across[1, slot] - update(cross[...], right0, 0))
        number = slot * grid_cols + me_col
        rest_rows = total - skipped
        updated = share[slot].reshape(total, width)[skipped:]
        updated -= update(left[0, skipped:, :], right0, 0) + update(left[1, skipped:, :], right1, 0)
        value = jnp.where(number == 0, left[0, skipped:, :], jnp.where(number == 1, left[1, skipped:, :], updated))
        staged[slot, skipped // rows_here :] = value.reshape(rest_rows // rows_here, rows_here, width)
        plain = 0.0 if skipped else jnp.where(me_row < PANELS, 0.0, updated[:rows_here])
        staged[slot, 0] = jnp.where(number == 0, first0, jnp.where(number == 1, first1, plain))
        out_copy(slot).start()

    for b in range(len(BLOCKS)):

        @pl.when(owners[b])
        def _(b=b):
            for n in range(len(grid_peers)):
                diag_copy(b, n).wait_send()

        for n in range(1, layers):
            pass_copy(b, n).wait_send()
    for k in range(PANELS):

        @pl.when(me_col == k)
        def _(k=k):
            for n in range(1, grid_cols):
                panel_copy(k, n).wait_send()

        @pl.when(me_row == k)
        def _(k=k):
            for slot in range(col_blocks):
                for n in range(1, grid_rows):
                    across_copy(k, slot, n).wait_send()
    for slot in range(col_blocks):
        out_copy(slot).wait()


def local(sizes, schur_window):
    layers, grid_rows, grid_cols, row_blocks, col_blocks, width = sizes
    rows_here = width // layers
    anywhere = pl.BlockSpec(memory_space=pl.ANY)
    dma = pltpu.SemaphoreType.DMA
    sends, diagonals, peers, half = len(BLOCKS), len({b[2] for b in BLOCKS}), grid_rows * grid_cols - 1, width // 2
    f32 = jnp.float32
    return pl.pallas_call(
        functools.partial(kernel, sizes),
        out_shape=jax.ShapeDtypeStruct((row_blocks, 1, rows_here, col_blocks, 1, width), f32),
        in_specs=[anywhere],
        out_specs=anywhere,
        scratch_shapes=[
            pltpu.VMEM((diagonals, width, width), f32),
            pltpu.VMEM((PANELS, col_blocks, width, width), f32),
            pltpu.VMEM((PANELS, row_blocks, rows_here, width), f32),
            pltpu.VMEM((col_blocks, row_blocks, rows_here, width), f32),
            pltpu.VMEM((col_blocks, row_blocks, rows_here, width), f32),
            pltpu.VMEM((half, width), f32),
            pltpu.VMEM((PANELS, width, width), f32),
            pltpu.VMEM((PANELS, width, width), f32),
            pltpu.VMEM((width, width), f32),
            pltpu.VMEM((width, width), f32),
            pltpu.VMEM((PANELS, row_blocks * rows_here, width), f32),
            dma((sends, peers)),
            dma((sends,)),
            dma((sends, layers - 1)),
            dma((sends, layers - 1)),
            dma((PANELS, col_blocks, grid_rows - 1)),
            dma((PANELS, col_blocks)),
            dma((PANELS, grid_cols - 1)),
            dma((PANELS,)),
            dma((sends,)),
            dma((col_blocks,)),
            dma((col_blocks,)),
        ],
        compiler_params=pltpu.CompilerParams(collective_id=0, has_side_effects=True),
        name="window",
    )(schur_window)


def solution(mesh):
    def body(schur_window):
        row_blocks, _, width, col_blocks, _, _ = schur_window.shape
        sizes = (mesh.shape["layer"], mesh.shape["row"], mesh.shape["col"], row_blocks, col_blocks, width)
        return local(sizes, schur_window)

    return jax.shard_map(
        body,
        mesh=mesh,
        in_specs=(P(None, "row", None, None, "col", None),),
        out_specs=P(None, "row", "layer", None, "col", None),
        check_vma=False,
    )
```
